32 devices in a mesh: clips: 2 (over y), ha: 4 (over z), ta: 2 (over x), wa: 2 (over core).
Axes of the slice: x: 2, y: 2, z: 4, core: 2. Of those that a mesh axis runs over, the one named last changes fastest.
Arguments:
- frames: bfloat16 [8, 16, 128, 192], P(('clips', 'ta'), 'ha', 'wa'), parts along dimension 0, may hold values from -6 to 6
- cache: bfloat16 [4, 16, 128, 192], P('clips', 'ha', 'wa'), parts along dimension 0, may hold values from -5 to 5
- norm_gain: float32 [192], replicated, may hold values from 0.25 to 1.75
- conv_weight: bfloat16 [3, 3, 3, 192, 192], replicated, may hold values from -0.078125 to 0.078125
- conv_bias: float32 [192], replicated, may hold values from -3 to 3
- up_weight: bfloat16 [3, 3, 192, 96], replicated, may hold values from -0.15625 to 0.15625
- up_bias: float32 [96], replicated, may hold values from -3 to 3
Outputs:
- upsampled: bfloat16 [8, 32, 128, 192], P(('clips', 'ta'), 'ha', 'wa'), parts along dimension 0
The draws below stay inside these ranges and needn't reach their ends.
There are 2 independent parts, one for each index of `clips`. The reference program is written for one: setup_inputs(seed, part) draws one part's arguments, and reference() takes and returns one part's arrays. A program takes and returns all parts, laid end to end along the dimension named above; an argument that names none is the same for every part. Nothing has to cross between parts.
All inputs are finite; a program needn't handle non-finite values.
Results may differ from the reference program's by a relative error of at most 0.0075.
Values may be sent and summed in bfloat16 or wider, within the bound.
A program may use at most 64 MiB of HBM per device.

```python
import jax
import jax.numpy as jnp
from jax import lax

C = 192
C_OUT = 96
FRAMES = 4
HEIGHT = 16
WIDTH = 128


def shard_levels(own_key, extent, split, least, top_value):
    level = 1.0
    for dim, shards_of in split:
        draws = jax.random.uniform(jax.random.fold_in(jax.random.fold_in(own_key, 6), dim), (shards_of,), jnp.float32, least / len(split), top_value / len(split))
        level = level * jnp.repeat(jnp.exp(draws), extent[dim] // shards_of).reshape((-1,) + (1,) * (len(extent) - 1 - dim))
    return level


def normal_values(stream_key, dims, spread, limit, shards=(), kind=jnp.bfloat16):
    drawn = spread * jax.random.normal(stream_key, dims, jnp.float32)
    if shards:
        drawn = drawn * shard_levels(stream_key, dims, shards, -0.22, 0.18)
    return jnp.clip(drawn, -limit, limit).astype(kind)


def setup_inputs(seed: int = 0, part: int = 0) -> dict:
    key_list = jax.random.split(jax.random.key(seed), 8)
    part_splits = jax.random.split(jax.random.fold_in(key_list[7], part), 8)
    return {
        "frames": normal_values(part_splits[0], (FRAMES, HEIGHT, WIDTH, C), 1.0, 6.0, ((0, 2), (1, 4), (2, 2))),
        "cache": normal_values(part_splits[1], (2, HEIGHT, WIDTH, C), 0.7, 5.0, ((1, 4), (2, 2))),
        "norm_gain": jnp.clip(1.0 + 0.15 * jax.random.normal(key_list[2], (C,), jnp.float32), 0.25, 1.75),
        "conv_weight": normal_values(key_list[3], (3, 3, 3, C, C), (27 * C) ** -0.5, 0.078125),
        "conv_bias": normal_values(key_list[4], (C,), 0.5, 3.0, (), jnp.float32),
        "up_weight": normal_values(key_list[5], (3, 3, C, C_OUT), (9 * C) ** -0.5, 0.15625),
        "up_bias": normal_values(key_list[6], (C_OUT,), 0.5, 3.0, (), jnp.float32),
    }


EPS = 1e-06

def activate(values, gain):
    wide = values.astype(jnp.float32)
    scale = lax.rsqrt(lax.optimization_barrier(jnp.mean(wide * wide, axis=-1, keepdims=True)) + EPS)
    return jax.nn.silu(wide * scale * gain).astype(jnp.bfloat16)

def causal_conv(padded, weight, count, rows, cols):
    channels = padded.shape[-1]
    total = jnp.zeros((count * rows * cols, weight.shape[-1]), jnp.float32)
    for a in range(3):
        for b in range(3):
            for c in range(3):
                window = padded[a:a + count, b:b + rows, c:c + cols].reshape(-1, channels)
                total = total + jnp.dot(window, weight[a, b, c], preferred_element_type=jnp.float32)
    return total.reshape(count, rows, cols, -1)

def upsample_conv(bordered, weight, bias):
    doubled = jnp.repeat(jnp.repeat(bordered, 2, axis=1), 2, axis=2)[:, 1:-1, 1:-1]
    count = doubled.shape[0]
    rows = doubled.shape[1] - 2
    cols = doubled.shape[2] - 2
    channels = doubled.shape[-1]
    total = jnp.zeros((count * rows * cols, weight.shape[-1]), jnp.float32)
    for a in range(3):
        for b in range(3):
            window = doubled[:, a:a + rows, b:b + cols].reshape(-1, channels)
            total = total + jnp.dot(window, weight[a, b], preferred_element_type=jnp.float32)
    result = (total + bias).astype(jnp.bfloat16)
    return result.reshape(count, rows, cols // 2, 2 * weight.shape[-1])

def reference(frames, cache, norm_gain, conv_weight, conv_bias, up_weight, up_bias):
    count, rows, cols, channels = frames.shape
    activated = activate(frames, norm_gain)
    extended = jnp.concatenate([cache, activated], axis=0)
    padded = jnp.pad(extended, ((0, 0), (1, 1), (1, 1), (0, 0)))
    convolved = causal_conv(padded, conv_weight, count, rows, cols)
    residual = (frames.astype(jnp.float32) + convolved + conv_bias).astype(jnp.bfloat16)
    bordered = jnp.pad(residual, ((0, 0), (1, 1), (1, 1), (0, 0)))
    return upsample_conv(bordered, up_weight, up_bias)
```

```python
import functools

import jax
import jax.numpy as jnp
from jax import lax
from jax.experimental import pallas as pl
from jax.experimental.pallas import tpu as pltpu
from jax.sharding import PartitionSpec as P

EPS = 1e-06
EDGE = 16
PHASE_TAPS = (((0, (0,)), (1, (1, 2))), ((1, (0, 1)), (2, (2,))))
F32 = jnp.float32
BF16 = jnp.bfloat16


class Move:
    def __init__(self, src, dst, sems, index, axis, by):
        here = lax.axis_index(axis)
        count = lax.axis_size(axis)
        self.can_send = jnp.logical_and(here + by >= 0, here + by < count)
        self.can_recv = jnp.logical_and(here - by >= 0, here - by < count)
        self.copy = lambda: pltpu.make_async_remote_copy(
            src_ref=src,
            dst_ref=dst,
            send_sem=sems[0].at[index],
            recv_sem=sems[1].at[index],
            device_id={axis: here + by},
            device_id_type=pl.DeviceIdType.MESH,
        )

    def start(self):
        pl.when(self.can_send)(lambda: self.copy().start())

    def recv(self):
        pl.when(self.can_recv)(lambda: self.copy().wait_recv())

    def sent(self):
        pl.when(self.can_send)(lambda: self.copy().wait_send())


def kernel(
    frames, cache, gain, weight, bias, up_weight, up_bias, out,
    fbuf, wbuf, ubuf, folded, ext, res, lbuf, rbuf, lbuf2, rbuf2, mid, low, high,
    local_sems, send_sems, recv_sems,
):
    count, rows, cols, channels = fbuf.shape
    wide = cols + EDGE
    outputs = ubuf.shape[-1]
    sems = (send_sems, recv_sems)
    here = {axis: lax.axis_index(axis) for axis in ("ta", "ha", "wa")}
    first = here["ta"] == 0
    ends = {
        "up": here["ha"] == 0,
        "down": here["ha"] == lax.axis_size("ha") - 1,
        "left": here["wa"] == 0,
        "right": here["wa"] == lax.axis_size("wa") - 1,
    }

    load_frames = pltpu.make_async_copy(frames, fbuf, local_sems.at[0])
    load_weight = pltpu.make_async_copy(weight, wbuf, local_sems.at[1])
    load_up = pltpu.make_async_copy(up_weight, ubuf, local_sems.at[2])
    load_cache = pltpu.make_async_copy(
        cache, ext.at[0:2, 1 : 1 + rows, 0:cols], local_sems.at[3]
    )
    load_frames.start()
    barrier = pltpu.get_barrier_semaphore()
    partners = jnp.int32(0)
    for axis in ("ta", "ha", "wa"):
        for by in (-1, 1):
            there = here[axis] + by
            valid = jnp.logical_and(there >= 0, there < lax.axis_size(axis))

            @pl.when(valid)
            def _():
                pl.semaphore_signal(
                    barrier, inc=1, device_id={axis: there},
                    device_id_type=pl.DeviceIdType.MESH,
                )

            partners = partners + valid.astype(jnp.int32)
    pl.when(first)(load_cache.start)
    load_weight.start()
    load_up.start()

    load_frames.wait()
    for f in range(count):
        for r in range(rows):
            x = fbuf[f, r].astype(F32)
            scale = lax.rsqrt(jnp.mean(x * x, axis=-1, keepdims=True) + EPS)
            v = x * scale * gain[...]
            ext[2 + f, 1 + r, 0:cols] = (v / (1.0 + jnp.exp(-v))).astype(BF16)

    @pl.when(ends["up"])
    def _():
        ext[:, 0, 0:cols] = jnp.zeros((2 + count, cols, channels), BF16)
        res[:, 0, 0:cols] = jnp.zeros((count, cols, channels), BF16)

    @pl.when(ends["down"])
    def _():
        ext[:, 1 + rows, 0:cols] = jnp.zeros((2 + count, cols, channels), BF16)
        res[:, 1 + rows, 0:cols] = jnp.zeros((count, cols, channels), BF16)

    index = 0

    def move(src, dst, axis, by):
        nonlocal index
        made = Move(src, dst, sems, index, axis, by)
        index += 1
        return made

    def row_moves(buf, lo, hi):
        return [
            move(buf.at[lo:hi, 1, 0:cols], buf.at[lo:hi, 1 + rows, 0:cols], "ha", -1),
            move(buf.at[lo:hi, rows, 0:cols], buf.at[lo:hi, 0, 0:cols], "ha", 1),
        ]

    def col_moves(buf, left, right, lo, hi):
        return [
            move(buf.at[lo:hi, :, 0:EDGE], right.at[lo:hi], "wa", -1),
            move(buf.at[lo:hi, :, cols - EDGE : cols], left.at[lo:hi], "wa", 1),
        ]

    def merge(buf, left, right, lo, hi):
        shape = (hi - lo, rows + 2, EDGE, channels)
        at = lax.broadcasted_iota(jnp.int32, shape, 2)
        from_right = jnp.logical_and(at == 0, jnp.logical_not(ends["right"]))
        from_left = jnp.logical_and(at == EDGE - 1, jnp.logical_not(ends["left"]))
        tile = jnp.where(from_left, left[lo:hi].astype(F32), 0.0)
        tile = jnp.where(from_right, right[lo:hi].astype(F32), tile)
        buf[lo:hi, :, cols:wide] = tile.astype(BF16)

    outer = {}
    inner = {}
    for f in (1, 0):
        outer[f] = [
            move(ext.at[2 + f, r, 0:cols], ext.at[f, r, 0:cols], "ta", 1)
            for r in (1, rows)
        ]
    for f in (1, 0):
        inner[f] = move(
            ext.at[2 + f, 2:rows, 0:cols], ext.at[f, 2:rows, 0:cols], "ta", 1
        )
    rows_of = {2: row_moves(ext, 2, 4), 1: row_moves(ext, 1, 2), 0: row_moves(ext, 0, 1)}
    cols_of = {
        2: col_moves(ext, lbuf, rbuf, 2, 4),
        1: col_moves(ext, lbuf, rbuf, 1, 2),
        0: col_moves(ext, lbuf, rbuf, 0, 1),
    }
    rows_res = row_moves(res, 0, count)
    cols_res = col_moves(res, lbuf2, rbuf2, 0, count)

    def each(moves, name):
        for m in moves:
            getattr(m, name)()

    def window(buf, f, start, width):
        return buf[f, start : start + rows, 0:width].reshape(rows * width, channels)

    def center(terms):
        total = None
        for f, a in terms:
            for b in range(3):
                part = jnp.dot(
                    window(ext, f, b, cols), wbuf[9 * a + 3 * b + 1],
                    preferred_element_type=F32,
                )
                total = part if total is None else total + part
        return total

    def side(terms, c):
        total = None
        for f, a in terms:
            for b in range(3):
                part = jnp.dot(
                    window(ext, f, b, wide), wbuf[9 * a + 3 * b + c],
                    preferred_element_type=F32,
                )
                total = part if total is None else total + part
        return total

    own = {0: ((2, 2),), 1: ((2, 1), (3, 2))}

    pl.semaphore_wait(barrier, partners)
    for f in (1, 0):
        each(outer[f], "start")
    each(rows_of[2], "start")
    for f in (1, 0):
        inner[f].start()

    load_up.wait()
    u = {}
    for a in range(3):
        for b in range(3):
            u[a, b] = ubuf[3 * a + b].astype(F32)
    for p in range(2):
        for k in range(2):
            taps = PHASE_TAPS[p][k][1]
            by_col = [functools.reduce(jnp.add, [u[a, b] for a in taps]) for b in range(3)]
            folded[p, k, 0] = jnp.concatenate(
                [by_col[1] + by_col[2], by_col[0] + by_col[1]], axis=-1
            ).astype(BF16)
            folded[p, k, 1] = jnp.concatenate([by_col[0], by_col[2]], axis=-1).astype(BF16)

    each(rows_of[2], "recv")
    each(cols_of[2], "start")
    load_weight.wait()
    for o in (0, 1):
        mid[o] = center(own[o])

    pl.when(first)(load_cache.wait)
    for f in (1, 0):
        each(outer[f], "recv")
        each(rows_of[f], "start")
    each(cols_of[2], "recv")
    merge(ext, lbuf, rbuf, 2, 4)
    for o in (0, 1):
        low[o] = side(own[o], 0)
        high[o] = side(own[o], 2)

    inner[1].recv()
    each(rows_of[1], "recv")
    each(cols_of[1], "start")
    inner[0].recv()
    each(rows_of[0], "recv")
    each(cols_of[0], "start")
    mid[0] += center(((1, 1), (0, 0)))
    mid[1] += center(((1, 0),))
    each(cols_of[1], "recv")
    each(cols_of[0], "recv")
    merge(ext, lbuf, rbuf, 0, 2)

    for o, terms in ((0, ((1, 1), (0, 0))), (1, ((1, 0),))):
        low[o] += side(terms, 0)
        high[o] += side(terms, 2)
        for r in range(rows):
            span = slice(r * wide, (r + 1) * wide)
            total = mid[o, r * cols : (r + 1) * cols]
            total = total + pltpu.roll(low[o, span], 1, 0)[0:cols]
            total = total + pltpu.roll(high[o, span], wide - 1, 0)[0:cols]
            res[o, 1 + r, 0:cols] = (fbuf[o, r].astype(F32) + total + bias[...]).astype(BF16)

    each(rows_res, "start")
    each(rows_res, "recv")
    each(cols_res, "start")
    up = jnp.concatenate([up_bias[...], up_bias[...]], axis=-1)
    lane = lax.broadcasted_iota(jnp.int32, (wide, 2 * outputs), 1)
    for o in range(count):
        for p in range(2):
            total = None
            for k in range(2):
                part = jnp.dot(
                    window(res, o, PHASE_TAPS[p][k][0], cols), folded[p, k, 0],
                    preferred_element_type=F32,
                )
                total = part if total is None else total + part
            if p == 0:
                mid[o] = total
            else:
                high[o, 0 : rows * cols] = total
    each(cols_res, "recv")
    merge(res, lbuf2, rbuf2, 0, count)
    for o in range(count):
        for p in range(2):
            total = None
            for k in range(2):
                part = jnp.dot(
                    window(res, o, PHASE_TAPS[p][k][0], wide), folded[p, k, 1],
                    preferred_element_type=F32,
                )
                total = part if total is None else total + part
            held = mid if p == 0 else high
            for r in range(rows):
                span = total[r * wide : (r + 1) * wide]
                turned = jnp.where(
                    lane < outputs, pltpu.roll(span, 1, 0), pltpu.roll(span, wide - 1, 0)
                )[0:cols]
                value = held[o, r * cols : (r + 1) * cols] + turned + up
                out[o, 2 * r + p] = value.astype(BF16)

    for f in (0, 1):
        each(outer[f], "sent")
        inner[f].sent()
    for f in (0, 1, 2):
        each(rows_of[f], "sent")
        each(cols_of[f], "sent")
    each(rows_res, "sent")
    each(cols_res, "sent")


def on_device(frames, cache, norm_gain, conv_weight, conv_bias, up_weight, up_bias):
    count, rows, cols, channels = frames.shape
    outputs = up_weight.shape[-1]
    wide = cols + EDGE
    moves = 22
    anywhere = pl.BlockSpec(memory_space=pl.ANY)
    vmem = pl.BlockSpec(memory_space=pltpu.VMEM)
    return pl.pallas_call(
        kernel,
        out_shape=jax.ShapeDtypeStruct((count, 2 * rows, cols, 2 * outputs), BF16),
        in_specs=[anywhere, anywhere, vmem, anywhere, vmem, anywhere, vmem],
        out_specs=vmem,
        scratch_shapes=[
            pltpu.VMEM((count, rows, cols, channels), BF16),
            pltpu.VMEM((27, channels, channels), BF16),
            pltpu.VMEM((9, channels, outputs), BF16),
            pltpu.VMEM((2, 2, 2, channels, 2 * outputs), BF16),
            pltpu.VMEM((2 + count, rows + 2, wide, channels), BF16),
            pltpu.VMEM((count, rows + 2, wide, channels), BF16),
            pltpu.VMEM((2 + count, rows + 2, EDGE, channels), BF16),
            pltpu.VMEM((2 + count, rows + 2, EDGE, channels), BF16),
            pltpu.VMEM((count, rows + 2, EDGE, channels), BF16),
            pltpu.VMEM((count, rows + 2, EDGE, channels), BF16),
            pltpu.VMEM((count, rows * cols, channels), F32),
            pltpu.VMEM((count, rows * wide, channels), F32),
            pltpu.VMEM((count, rows * wide, channels), F32),
            pltpu.SemaphoreType.DMA((4,)),
            pltpu.SemaphoreType.DMA((moves,)),
            pltpu.SemaphoreType.DMA((moves,)),
        ],
        compiler_params=pltpu.CompilerParams(
            collective_id=0, has_side_effects=True, vmem_limit_bytes=48 * 1024 * 1024
        ),
        name="level",
    )(
        frames,
        cache,
        norm_gain.reshape(1, channels),
        conv_weight.reshape(27, channels, channels),
        conv_bias.reshape(1, channels),
        up_weight.reshape(9, channels, outputs),
        up_bias.reshape(1, outputs),
    )


def solution(mesh):
    return jax.shard_map(
        on_device,
        mesh=mesh,
        in_specs=(
            P(("clips", "ta"), "ha", "wa", None),
            P("clips", "ha", "wa", None),
            P(),
            P(),
            P(),
            P(),
            P(),
        ),
        out_specs=P(("clips", "ta"), "ha", "wa", None),
        check_vma=False,
    )
```

```python
import functools

import jax
import jax.numpy as jnp
from jax import lax
from jax.experimental import pallas as pl
from jax.experimental.pallas import tpu as pltpu
from jax.sharding import PartitionSpec as P

EPS = 1e-06
EDGE = 16
PHASE_TAPS = (((0, (0,)), (1, (1, 2))), ((1, (0, 1)), (2, (2,))))
F32 = jnp.float32
BF16 = jnp.bfloat16


class Move:
    def __init__(self, src, dst, sems, index, axis, by):
        here = lax.axis_index(axis)
        count = lax.axis_size(axis)
        self.can_send = jnp.logical_and(here + by >= 0, here + by < count)
        self.can_recv = jnp.logical_and(here - by >= 0, here - by < count)
        self.copy = lambda: pltpu.make_async_remote_copy(
            src_ref=src,
            dst_ref=dst,
            send_sem=sems[0].at[index],
            recv_sem=sems[1].at[index],
            device_id={axis: here + by},
            device_id_type=pl.DeviceIdType.MESH,
        )

    def start(self):
        pl.when(self.can_send)(lambda: self.copy().start())

    def recv(self):
        pl.when(self.can_recv)(lambda: self.copy().wait_recv())

    def sent(self):
        pl.when(self.can_send)(lambda: self.copy().wait_send())


def kernel(
    frames, cache, gain_in, weight, bias_in, up_weight, up_bias_in, out,
    fbuf, wbuf, ubuf, gain, bias, up_bias, folded, ext, res, lbuf, rbuf, lbuf2, rbuf2, mid, low, high,
    local_sems, send_sems, recv_sems,
):
    count, rows, cols, channels = fbuf.shape
    wide = cols + EDGE
    outputs = ubuf.shape[-1]
    sems = (send_sems, recv_sems)
    here = {axis: lax.axis_index(axis) for axis in ("ta", "ha", "wa")}
    first = here["ta"] == 0
    ends = {
        "up": here["ha"] == 0,
        "down": here["ha"] == lax.axis_size("ha") - 1,
        "left": here["wa"] == 0,
        "right": here["wa"] == lax.axis_size("wa") - 1,
    }

    load_frames = pltpu.make_async_copy(frames, fbuf, local_sems.at[0])
    load_weight = pltpu.make_async_copy(weight, wbuf, local_sems.at[1])
    load_up = pltpu.make_async_copy(up_weight, ubuf, local_sems.at[2])
    load_cache = pltpu.make_async_copy(
        cache, ext.at[0:2, 1 : 1 + rows, 0:cols], local_sems.at[3]
    )
    load_gain = pltpu.make_async_copy(gain_in, gain, local_sems.at[4])
    load_bias = pltpu.make_async_copy(bias_in, bias, local_sems.at[5])
    load_up_bias = pltpu.make_async_copy(up_bias_in, up_bias, local_sems.at[6])
    load_frames.start()
    load_gain.start()
    barrier = pltpu.get_barrier_semaphore()
    partners = jnp.int32(0)
    for axis in ("ta", "ha", "wa"):
        for by in (-1, 1):
            there = here[axis] + by
            valid = jnp.logical_and(there >= 0, there < lax.axis_size(axis))

            @pl.when(valid)
            def _():
                pl.semaphore_signal(
                    barrier, inc=1, device_id={axis: there},
                    device_id_type=pl.DeviceIdType.MESH,
                )

            partners = partners + valid.astype(jnp.int32)
    pl.when(first)(load_cache.start)
    load_weight.start()
    load_up.start()
    load_bias.start()
    load_up_bias.start()

    load_gain.wait()
    load_frames.wait()
    for f in range(count):
        for r in range(rows):
            x = fbuf[f, r].astype(F32)
            scale = lax.rsqrt(jnp.mean(x * x, axis=-1, keepdims=True) + EPS)
            v = x * scale * gain[...]
            ext[2 + f, 1 + r, 0:cols] = (v / (1.0 + jnp.exp(-v))).astype(BF16)

    @pl.when(ends["up"])
    def _():
        ext[:, 0, 0:cols] = jnp.zeros((2 + count, cols, channels), BF16)
        res[:, 0, 0:cols] = jnp.zeros((count, cols, channels), BF16)

    @pl.when(ends["down"])
    def _():
        ext[:, 1 + rows, 0:cols] = jnp.zeros((2 + count, cols, channels), BF16)
        res[:, 1 + rows, 0:cols] = jnp.zeros((count, cols, channels), BF16)

    index = 0

    def move(src, dst, axis, by):
        nonlocal index
        made = Move(src, dst, sems, index, axis, by)
        index += 1
        return made

    def row_moves(buf, lo, hi):
        return [
            move(buf.at[lo:hi, 1, 0:cols], buf.at[lo:hi, 1 + rows, 0:cols], "ha", -1),
            move(buf.at[lo:hi, rows, 0:cols], buf.at[lo:hi, 0, 0:cols], "ha", 1),
        ]

    def col_moves(buf, left, right, lo, hi):
        return [
            move(buf.at[lo:hi, :, 0:EDGE], right.at[lo:hi], "wa", -1),
            move(buf.at[lo:hi, :, cols - EDGE : cols], left.at[lo:hi], "wa", 1),
        ]

    def merge(buf, left, right, lo, hi):
        shape = (hi - lo, rows + 2, EDGE, channels)
        at = lax.broadcasted_iota(jnp.int32, shape, 2)
        from_right = jnp.logical_and(at == 0, jnp.logical_not(ends["right"]))
        from_left = jnp.logical_and(at == EDGE - 1, jnp.logical_not(ends["left"]))
        tile = jnp.where(from_left, left[lo:hi].astype(F32), 0.0)
        tile = jnp.where(from_right, right[lo:hi].astype(F32), tile)
        buf[lo:hi, :, cols:wide] = tile.astype(BF16)

    outer = {}
    inner = {}
    for f in (1, 0):
        outer[f] = [
            move(ext.at[2 + f, r, 0:cols], ext.at[f, r, 0:cols], "ta", 1)
            for r in (1, rows)
        ]
    for f in (1, 0):
        inner[f] = move(
            ext.at[2 + f, 2:rows, 0:cols], ext.at[f, 2:rows, 0:cols], "ta", 1
        )
    rows_of = {2: row_moves(ext, 2, 4), 1: row_moves(ext, 1, 2), 0: row_moves(ext, 0, 1)}
    cols_of = {
        2: col_moves(ext, lbuf, rbuf, 2, 4),
        1: col_moves(ext, lbuf, rbuf, 1, 2),
        0: col_moves(ext, lbuf, rbuf, 0, 1),
    }
    rows_res = row_moves(res, 0, count)
    cols_res = col_moves(res, lbuf2, rbuf2, 0, count)

    def each(moves, name):
        for m in moves:
            getattr(m, name)()

    def window(buf, f, start, width):
        return buf[f, start : start + rows, 0:width].reshape(rows * width, channels)

    def center(terms):
        total = None
        for f, a in terms:
            for b in range(3):
                part = jnp.dot(
                    window(ext, f, b, cols), wbuf[9 * a + 3 * b + 1],
                    preferred_element_type=F32,
                )
                total = part if total is None else total + part
        return total

    def side(terms, c):
        total = None
        for f, a in terms:
            for b in range(3):
                part = jnp.dot(
                    window(ext, f, b, wide), wbuf[9 * a + 3 * b + c],
                    preferred_element_type=F32,
                )
                total = part if total is None else total + part
        return total

    own = {0: ((2, 2),), 1: ((2, 1), (3, 2))}

    pl.semaphore_wait(barrier, partners)
    for f in (1, 0):
        each(outer[f], "start")
    each(rows_of[2], "start")
    for f in (1, 0):
        inner[f].start()

    load_up.wait()
    load_bias.wait()
    load_up_bias.wait()
    u = {}
    for a in range(3):
        for b in range(3):
            u[a, b] = ubuf[3 * a + b].astype(F32)
    for p in range(2):
        for k in range(2):
            taps = PHASE_TAPS[p][k][1]
            by_col = [functools.reduce(jnp.add, [u[a, b] for a in taps]) for b in range(3)]
            folded[p, k, 0] = jnp.concatenate(
                [by_col[1] + by_col[2], by_col[0] + by_col[1]], axis=-1
            ).astype(BF16)
            folded[p, k, 1] = jnp.concatenate([by_col[0], by_col[2]], axis=-1).astype(BF16)

    each(rows_of[2], "recv")
    each(cols_of[2], "start")
    load_weight.wait()
    for o in (0, 1):
        mid[o] = center(own[o])

    pl.when(first)(load_cache.wait)
    for f in (1, 0):
        each(outer[f], "recv")
        each(rows_of[f], "start")
    each(cols_of[2], "recv")
    merge(ext, lbuf, rbuf, 2, 4)
    for o in (0, 1):
        low[o] = side(own[o], 0)
        high[o] = side(own[o], 2)

    inner[1].recv()
    each(rows_of[1], "recv")
    each(cols_of[1], "start")
    inner[0].recv()
    each(rows_of[0], "recv")
    each(cols_of[0], "start")
    mid[0] += center(((1, 1), (0, 0)))
    mid[1] += center(((1, 0),))
    each(cols_of[1], "recv")
    each(cols_of[0], "recv")
    merge(ext, lbuf, rbuf, 0, 2)

    for o, terms in ((0, ((1, 1), (0, 0))), (1, ((1, 0),))):
        low[o] += side(terms, 0)
        high[o] += side(terms, 2)
        for r in range(rows):
            span = slice(r * wide, (r + 1) * wide)
            total = mid[o, r * cols : (r + 1) * cols]
            total = total + pltpu.roll(low[o, span], 1, 0)[0:cols]
            total = total + pltpu.roll(high[o, span], wide - 1, 0)[0:cols]
            res[o, 1 + r, 0:cols] = (fbuf[o, r].astype(F32) + total + bias[...]).astype(BF16)

    each(rows_res, "start")
    each(rows_res, "recv")
    each(cols_res, "start")
    up = jnp.concatenate([up_bias[...], up_bias[...]], axis=-1)
    lane = lax.broadcasted_iota(jnp.int32, (wide, 2 * outputs), 1)
    for o in range(count):
        for p in range(2):
            total = None
            for k in range(2):
                part = jnp.dot(
                    window(res, o, PHASE_TAPS[p][k][0], cols), folded[p, k, 0],
                    preferred_element_type=F32,
                )
                total = part if total is None else total + part
            if p == 0:
                mid[o] = total
            else:
                high[o, 0 : rows * cols] = total
    each(cols_res, "recv")
    merge(res, lbuf2, rbuf2, 0, count)
    for o in range(count):
        for p in range(2):
            total = None
            for k in range(2):
                part = jnp.dot(
                    window(res, o, PHASE_TAPS[p][k][0], wide), folded[p, k, 1],
                    preferred_element_type=F32,
                )
                total = part if total is None else total + part
            held = mid if p == 0 else high
            for r in range(rows):
                span = total[r * wide : (r + 1) * wide]
                turned = jnp.where(
                    lane < outputs, pltpu.roll(span, 1, 0), pltpu.roll(span, wide - 1, 0)
                )[0:cols]
                value = held[o, r * cols : (r + 1) * cols] + turned + up
                out[o, 2 * r + p] = value.astype(BF16)

    for f in (0, 1):
        each(outer[f], "sent")
        inner[f].sent()
    for f in (0, 1, 2):
        each(rows_of[f], "sent")
        each(cols_of[f], "sent")
    each(rows_res, "sent")
    each(cols_res, "sent")


def on_device(frames, cache, norm_gain, conv_weight, conv_bias, up_weight, up_bias):
    count, rows, cols, channels = frames.shape
    outputs = up_weight.shape[-1]
    wide = cols + EDGE
    moves = 22
    hbm = pl.BlockSpec(memory_space=pltpu.HBM)
    vmem = pl.BlockSpec(memory_space=pltpu.VMEM)
    return pl.pallas_call(
        kernel,
        out_shape=jax.ShapeDtypeStruct((count, 2 * rows, cols, 2 * outputs), BF16),
        in_specs=[hbm] * 7,
        out_specs=vmem,
        scratch_shapes=[
            pltpu.VMEM((count, rows, cols, channels), BF16),
            pltpu.VMEM((27, channels, channels), BF16),
            pltpu.VMEM((9, channels, outputs), BF16),
            pltpu.VMEM((1, channels), F32),
            pltpu.VMEM((1, channels), F32),
            pltpu.VMEM((1, outputs), F32),
            pltpu.VMEM((2, 2, 2, channels, 2 * outputs), BF16),
            pltpu.VMEM((2 + count, rows + 2, wide, channels), BF16),
            pltpu.VMEM((count, rows + 2, wide, channels), BF16),
            pltpu.VMEM((2 + count, rows + 2, EDGE, channels), BF16),
            pltpu.VMEM((2 + count, rows + 2, EDGE, channels), BF16),
            pltpu.VMEM((count, rows + 2, EDGE, channels), BF16),
            pltpu.VMEM((count, rows + 2, EDGE, channels), BF16),
            pltpu.VMEM((count, rows * cols, channels), F32),
            pltpu.VMEM((count, rows * wide, channels), F32),
            pltpu.VMEM((count, rows * wide, channels), F32),
            pltpu.SemaphoreType.DMA((7,)),
            pltpu.SemaphoreType.DMA((moves,)),
            pltpu.SemaphoreType.DMA((moves,)),
        ],
        compiler_params=pltpu.CompilerParams(
            collective_id=0, has_side_effects=True, vmem_limit_bytes=48 * 1024 * 1024
        ),
        name="level",
    )(
        frames,
        cache,
        norm_gain.reshape(1, channels),
        conv_weight.reshape(27, channels, channels),
        conv_bias.reshape(1, channels),
        up_weight.reshape(9, channels, outputs),
        up_bias.reshape(1, outputs),
    )


def solution(mesh):
    return jax.shard_map(
        on_device,
        mesh=mesh,
        in_specs=(
            P(("clips", "ta"), "ha", "wa", None),
            P("clips", "ha", "wa", None),
            P(),
            P(),
            P(),
            P(),
            P(),
        ),
        out_specs=P(("clips", "ta"), "ha", "wa", None),
        check_vma=False,
    )
```

```python
import functools

import jax
import jax.numpy as jnp
from jax import lax
from jax.experimental import pallas as pl
from jax.experimental.pallas import tpu as pltpu
from jax.sharding import PartitionSpec as P

EPS = 1e-06
EDGE = 16
PHASE_TAPS = (((0, (0,)), (1, (1, 2))), ((1, (0, 1)), (2, (2,))))
NEIGHBOURS = (
    {"ta": 1}, {"ta": -1}, {"ha": 1}, {"ha": -1}, {"wa": 1}, {"wa": -1},
    {"ha": 1, "wa": 1}, {"ha": 1, "wa": -1}, {"ha": -1, "wa": 1}, {"ha": -1, "wa": -1},
)
F32 = jnp.float32
BF16 = jnp.bfloat16


def reachable(by, sign):
    found = None
    for axis, step in by.items():
        there = lax.axis_index(axis) + sign * step
        inside = jnp.logical_and(there >= 0, there < lax.axis_size(axis))
        found = inside if found is None else jnp.logical_and(found, inside)
    return found


class Move:
    def __init__(self, src, dst, sems, index, by):
        self.can_send = reachable(by, 1)
        self.can_recv = reachable(by, -1)
        self.copy = lambda: pltpu.make_async_remote_copy(
            src_ref=src,
            dst_ref=dst,
            send_sem=sems[0].at[index],
            recv_sem=sems[1].at[index],
            device_id={axis: lax.axis_index(axis) + step for axis, step in by.items()},
            device_id_type=pl.DeviceIdType.MESH,
        )

    def start(self):
        pl.when(self.can_send)(lambda: self.copy().start())

    def recv(self):
        pl.when(self.can_recv)(lambda: self.copy().wait_recv())

    def sent(self):
        pl.when(self.can_send)(lambda: self.copy().wait_send())


def kernel(
    frames, cache, gain_in, weight, bias_in, up_weight, up_bias_in, out,
    fbuf, wbuf, ubuf, gain, bias, up_bias, folded, ext, res, lbuf, rbuf, lbuf2, rbuf2, mid, low, high, obuf,
    local_sems, send_sems, recv_sems,
):
    count, rows, cols, channels = fbuf.shape
    wide = cols + EDGE
    outputs = ubuf.shape[-1]
    sems = (send_sems, recv_sems)
    here = {axis: lax.axis_index(axis) for axis in ("ta", "ha", "wa")}
    first = here["ta"] == 0
    ends = {
        "up": here["ha"] == 0,
        "down": here["ha"] == lax.axis_size("ha") - 1,
        "left": here["wa"] == 0,
        "right": here["wa"] == lax.axis_size("wa") - 1,
    }

    load_frames = pltpu.make_async_copy(frames, fbuf, local_sems.at[0])
    load_weight = pltpu.make_async_copy(weight, wbuf, local_sems.at[1])
    load_up = pltpu.make_async_copy(up_weight, ubuf, local_sems.at[2])
    load_cache = pltpu.make_async_copy(
        cache, ext.at[0:2, 1 : 1 + rows, 0:cols], local_sems.at[3]
    )
    load_gain = pltpu.make_async_copy(gain_in, gain, local_sems.at[4])
    load_bias = pltpu.make_async_copy(bias_in, bias, local_sems.at[5])
    load_up_bias = pltpu.make_async_copy(up_bias_in, up_bias, local_sems.at[6])
    load_frames.start()
    load_gain.start()
    barrier = pltpu.get_barrier_semaphore()
    partners = jnp.int32(0)
    for by in NEIGHBOURS:
        valid = reachable(by, 1)

        @pl.when(valid)
        def _():
            pl.semaphore_signal(
                barrier, inc=1,
                device_id={axis: here[axis] + step for axis, step in by.items()},
                device_id_type=pl.DeviceIdType.MESH,
            )

        partners = partners + valid.astype(jnp.int32)
    pl.when(first)(load_cache.start)
    load_weight.start()
    load_up.start()
    load_bias.start()
    load_up_bias.start()

    load_gain.wait()
    load_frames.wait()
    for f in range(count):
        for r in range(rows):
            x = fbuf[f, r].astype(F32)
            scale = lax.rsqrt(jnp.mean(x * x, axis=-1, keepdims=True) + EPS)
            v = x * scale * gain[...]
            ext[2 + f, 1 + r, 0:cols] = (v / (1.0 + jnp.exp(-v))).astype(BF16)

    @pl.when(ends["up"])
    def _():
        ext[:, 0, 0:cols] = jnp.zeros((2 + count, cols, channels), BF16)
        res[:, 0, 0:cols] = jnp.zeros((count, cols, channels), BF16)

    @pl.when(ends["down"])
    def _():
        ext[:, 1 + rows, 0:cols] = jnp.zeros((2 + count, cols, channels), BF16)
        res[:, 1 + rows, 0:cols] = jnp.zeros((count, cols, channels), BF16)

    index = 0

    def move(src, dst, by):
        nonlocal index
        made = Move(src, dst, sems, index, by)
        index += 1
        return made

    last = cols - EDGE

    def edges(buf, left, right, lo, hi):
        inside = slice(1, 1 + rows)
        near = slice(0, EDGE)
        far = slice(last, cols)
        across = [
            move(buf.at[lo:hi, 1, 0:cols], buf.at[lo:hi, 1 + rows, 0:cols], {"ha": -1}),
            move(buf.at[lo:hi, rows, 0:cols], buf.at[lo:hi, 0, 0:cols], {"ha": 1}),
        ]
        beside = [
            move(buf.at[lo:hi, 1, near], right.at[lo:hi, 1 + rows], {"ha": -1, "wa": -1}),
            move(buf.at[lo:hi, 1, far], left.at[lo:hi, 1 + rows], {"ha": -1, "wa": 1}),
            move(buf.at[lo:hi, rows, near], right.at[lo:hi, 0], {"ha": 1, "wa": -1}),
            move(buf.at[lo:hi, rows, far], left.at[lo:hi, 0], {"ha": 1, "wa": 1}),
            move(buf.at[lo:hi, inside, near], right.at[lo:hi, inside], {"wa": -1}),
            move(buf.at[lo:hi, inside, far], left.at[lo:hi, inside], {"wa": 1}),
        ]
        return across, beside

    def merge(buf, left, right, lo, hi):
        shape = (hi - lo, rows + 2, EDGE, channels)
        row = lax.broadcasted_iota(jnp.int32, shape, 1)
        at = lax.broadcasted_iota(jnp.int32, shape, 2)
        top = jnp.where(ends["up"], 1, 0)
        end = jnp.where(ends["down"], rows, rows + 1)
        held = jnp.logical_and(row >= top, row <= end)
        near = jnp.where(ends["right"], -1, 0)
        far = jnp.where(ends["left"], -1, EDGE - 1)
        tile = jnp.where(jnp.logical_and(held, at == far), left[lo:hi].astype(F32), 0.0)
        tile = jnp.where(jnp.logical_and(held, at == near), right[lo:hi].astype(F32), tile)
        buf[lo:hi, :, cols:wide] = tile.astype(BF16)

    def later(at, row, col):
        return move(ext.at[(at[0],) + (row, col)], ext.at[(at[1],) + (row, col)], {"ta": 1})

    both = (slice(2, 4), slice(0, 2))
    outer = [
        later(both, 1, slice(0, cols)),
        later(both, rows, slice(0, cols)),
        later(both, slice(2, rows), slice(0, EDGE)),
        later(both, slice(2, rows), slice(last, cols)),
    ]
    inner = {f: later((2 + f, f), slice(2, rows), slice(EDGE, last)) for f in (1, 0)}
    across_own, beside_own = edges(ext, lbuf, rbuf, 2, 4)
    across_old, beside_old = edges(ext, lbuf, rbuf, 0, 2)
    across_res, beside_res = {}, {}
    for o in (1, 0):
        across_res[o], beside_res[o] = edges(res, lbuf2, rbuf2, o, o + 1)

    def each(moves, name):
        for m in moves:
            getattr(m, name)()

    def window(buf, f, start, width):
        return buf[f, start : start + rows, 0:width].reshape(rows * width, channels)

    def center(terms):
        total = None
        for f, a in terms:
            for b in range(3):
                part = jnp.dot(
                    window(ext, f, b, cols), wbuf[9 * a + 3 * b + 1],
                    preferred_element_type=F32,
                )
                total = part if total is None else total + part
        return total

    def side(terms, c):
        total = None
        for f, a in terms:
            for b in range(3):
                part = jnp.dot(
                    window(ext, f, b, wide), wbuf[9 * a + 3 * b + c],
                    preferred_element_type=F32,
                )
                total = part if total is None else total + part
        return total

    own = {0: ((2, 2),), 1: ((2, 1), (3, 2))}

    pl.semaphore_wait(barrier, partners)
    each(outer, "start")
    each(across_own, "start")
    each(beside_own, "start")
    for f in (1, 0):
        inner[f].start()

    load_up.wait()
    load_bias.wait()
    load_up_bias.wait()
    u = {}
    for a in range(3):
        for b in range(3):
            u[a, b] = ubuf[3 * a + b].astype(F32)
    for p in range(2):
        for k in range(2):
            taps = PHASE_TAPS[p][k][1]
            by_col = [functools.reduce(jnp.add, [u[a, b] for a in taps]) for b in range(3)]
            folded[p, k, 0] = jnp.concatenate(
                [by_col[1] + by_col[2], by_col[0] + by_col[1]], axis=-1
            ).astype(BF16)
            folded[p, k, 1] = jnp.concatenate([by_col[0], by_col[2]], axis=-1).astype(BF16)

    load_weight.wait()
    each(across_own, "recv")
    for o in (1, 0):
        mid[o] = center(own[o])
    each(beside_own, "recv")
    merge(ext, lbuf, rbuf, 2, 4)
    low[1] = side(own[1], 0)
    high[1] = side(own[1], 2)

    pl.when(first)(load_cache.wait)
    each(outer, "recv")
    each(across_old, "start")
    each(beside_old, "start")
    low[0] = side(own[0], 0)
    high[0] = side(own[0], 2)

    def finish(o, center_sum, low_sum, high_sum):
        for r in range(rows):
            span = slice(r * wide, (r + 1) * wide)
            total = center_sum[r * cols : (r + 1) * cols]
            total = total + pltpu.roll(low_sum[span], 1, 0)[0:cols]
            total = total + pltpu.roll(high_sum[span], wide - 1, 0)[0:cols]
            res[o, 1 + r, 0:cols] = (fbuf[o, r].astype(F32) + total + bias[...]).astype(BF16)

    inner[1].recv()
    each(across_old, "recv")
    mid[1] += center(((1, 0),))
    each(beside_old, "recv")
    merge(ext, lbuf, rbuf, 0, 2)
    low[1] += side(((1, 0),), 0)
    high[1] += side(((1, 0),), 2)
    finish(1, mid.at[1], low.at[1], high.at[1])
    each(across_res[1], "start")
    each(beside_res[1], "start")

    inner[0].recv()
    mid[0] += center(((1, 1), (0, 0)))
    low[0] += side(((1, 1), (0, 0)), 0)
    high[0] += side(((1, 1), (0, 0)), 2)
    finish(0, mid.at[0], low.at[0], high.at[0])
    each(across_res[0], "start")
    each(beside_res[0], "start")

    up = jnp.concatenate([up_bias[...], up_bias[...]], axis=-1)
    lane = lax.broadcasted_iota(jnp.int32, (wide, 2 * outputs), 1)

    def raised(o, p, kind, width):
        total = None
        for k in range(2):
            part = jnp.dot(
                window(res, o, PHASE_TAPS[p][k][0], width), folded[p, k, kind],
                preferred_element_type=F32,
            )
            total = part if total is None else total + part
        return total

    stores = {o: pltpu.make_async_copy(obuf.at[o], out.at[o], local_sems.at[7 + o]) for o in (1, 0)}
    for o in (1, 0):
        each(across_res[o], "recv")
        mid[o] = raised(o, 0, 0, cols)
        high[o, 0 : rows * cols] = raised(o, 1, 0, cols)
        each(beside_res[o], "recv")
        merge(res, lbuf2, rbuf2, o, o + 1)
        for p in range(2):
            total = raised(o, p, 1, wide)
            held = mid if p == 0 else high
            for r in range(rows):
                span = total[r * wide : (r + 1) * wide]
                turned = jnp.where(
                    lane < outputs, pltpu.roll(span, 1, 0), pltpu.roll(span, wide - 1, 0)
                )[0:cols]
                value = held[o, r * cols : (r + 1) * cols] + turned + up
                obuf[o, 2 * r + p] = value.astype(BF16)
        stores[o].start()

    each(outer, "sent")
    for f in (1, 0):
        inner[f].sent()
    for moves in (across_own, beside_own, across_old, beside_old):
        each(moves, "sent")
    for o in (1, 0):
        each(across_res[o], "sent")
        each(beside_res[o], "sent")
        stores[o].wait()


def on_device(frames, cache, norm_gain, conv_weight, conv_bias, up_weight, up_bias):
    count, rows, cols, channels = frames.shape
    outputs = up_weight.shape[-1]
    wide = cols + EDGE
    moves = 38
    hbm = pl.BlockSpec(memory_space=pltpu.HBM)
    return pl.pallas_call(
        kernel,
        out_shape=jax.ShapeDtypeStruct((count, 2 * rows, cols, 2 * outputs), BF16),
        in_specs=[hbm] * 7,
        out_specs=hbm,
        scratch_shapes=[
            pltpu.VMEM((count, rows, cols, channels), BF16),
            pltpu.VMEM((27, channels, channels), BF16),
            pltpu.VMEM((9, channels, outputs), BF16),
            pltpu.VMEM((1, channels), F32),
            pltpu.VMEM((1, channels), F32),
            pltpu.VMEM((1, outputs), F32),
            pltpu.VMEM((2, 2, 2, channels, 2 * outputs), BF16),
            pltpu.VMEM((2 + count, rows + 2, wide, channels), BF16),
            pltpu.VMEM((count, rows + 2, wide, channels), BF16),
            pltpu.VMEM((2 + count, rows + 2, EDGE, channels), BF16),
            pltpu.VMEM((2 + count, rows + 2, EDGE, channels), BF16),
            pltpu.VMEM((count, rows + 2, EDGE, channels), BF16),
            pltpu.VMEM((count, rows + 2, EDGE, channels), BF16),
            pltpu.VMEM((count, rows * cols, channels), F32),
            pltpu.VMEM((count, rows * wide, channels), F32),
            pltpu.VMEM((count, rows * wide, channels), F32),
            pltpu.VMEM((count, 2 * rows, cols, 2 * outputs), BF16),
            pltpu.SemaphoreType.DMA((9,)),
            pltpu.SemaphoreType.DMA((moves,)),
            pltpu.SemaphoreType.DMA((moves,)),
        ],
        compiler_params=pltpu.CompilerParams(
            collective_id=0, has_side_effects=True, vmem_limit_bytes=65_000_000
        ),
        name="level",
    )(
        frames,
        cache,
        norm_gain.reshape(1, channels),
        conv_weight.reshape(27, channels, channels),
        conv_bias.reshape(1, channels),
        up_weight.reshape(9, channels, outputs),
        up_bias.reshape(1, outputs),
    )


def solution(mesh):
    return jax.shard_map(
        on_device,
        mesh=mesh,
        in_specs=(
            P(("clips", "ta"), "ha", "wa", None),
            P("clips", "ha", "wa", None),
            P(),
            P(),
            P(),
            P(),
            P(),
        ),
        out_specs=P(("clips", "ta"), "ha", "wa", None),
        check_vma=False,
    )
```

```python
import functools

import jax
import jax.numpy as jnp
from jax import lax
from jax.experimental import pallas as pl
from jax.experimental.pallas import tpu as pltpu
from jax.sharding import PartitionSpec as P

EPS = 1e-06
EDGE = 16
PHASE_TAPS = (((0, (0,)), (1, (1, 2))), ((1, (0, 1)), (2, (2,))))
NEIGHBOURS = (
    {"ta": 1}, {"ta": -1}, {"ha": 1}, {"ha": -1}, {"wa": 1}, {"wa": -1},
    {"ha": 1, "wa": 1}, {"ha": 1, "wa": -1}, {"ha": -1, "wa": 1}, {"ha": -1, "wa": -1},
)
F32 = jnp.float32
BF16 = jnp.bfloat16


def reachable(by, sign):
    found = None
    for axis, step in by.items():
        there = lax.axis_index(axis) + sign * step
        inside = jnp.logical_and(there >= 0, there < lax.axis_size(axis))
        found = inside if found is None else jnp.logical_and(found, inside)
    return found


class Move:
    def __init__(self, src, dst, sems, index, by):
        self.can_send = reachable(by, 1)
        self.can_recv = reachable(by, -1)
        self.copy = lambda: pltpu.make_async_remote_copy(
            src_ref=src,
            dst_ref=dst,
            send_sem=sems[0].at[index],
            recv_sem=sems[1].at[index],
            device_id={axis: lax.axis_index(axis) + step for axis, step in by.items()},
            device_id_type=pl.DeviceIdType.MESH,
        )

    def start(self):
        pl.when(self.can_send)(lambda: self.copy().start())

    def recv(self):
        pl.when(self.can_recv)(lambda: self.copy().wait_recv())

    def sent(self):
        pl.when(self.can_send)(lambda: self.copy().wait_send())


def kernel(
    frames, cache, gain_in, weight, bias_in, up_weight, up_bias_in, out,
    fbuf, wbuf, ubuf, gain, bias, up_bias, folded, ext, res, lbuf, rbuf, lbuf2, rbuf2, mid, low, high, obuf,
    local_sems, send_sems, recv_sems,
):
    count, rows, cols, channels = fbuf.shape
    wide = cols + EDGE
    outputs = ubuf.shape[-1]
    sems = (send_sems, recv_sems)
    here = {axis: lax.axis_index(axis) for axis in ("ta", "ha", "wa")}
    first = here["ta"] == 0
    ends = {
        "up": here["ha"] == 0,
        "down": here["ha"] == lax.axis_size("ha") - 1,
        "left": here["wa"] == 0,
        "right": here["wa"] == lax.axis_size("wa") - 1,
    }

    load_frames = pltpu.make_async_copy(frames, fbuf, local_sems.at[0])
    load_weight = pltpu.make_async_copy(weight, wbuf, local_sems.at[1])
    load_up = pltpu.make_async_copy(up_weight, ubuf, local_sems.at[2])
    load_cache = pltpu.make_async_copy(
        cache, ext.at[0:2, 1 : 1 + rows, 0:cols], local_sems.at[3]
    )
    load_gain = pltpu.make_async_copy(gain_in, gain, local_sems.at[4])
    load_bias = pltpu.make_async_copy(bias_in, bias, local_sems.at[5])
    load_up_bias = pltpu.make_async_copy(up_bias_in, up_bias, local_sems.at[6])
    load_frames.start()
    load_gain.start()
    barrier = pltpu.get_barrier_semaphore()
    partners = jnp.int32(0)
    for by in NEIGHBOURS:
        valid = reachable(by, 1)

        @pl.when(valid)
        def _():
            pl.semaphore_signal(
                barrier, inc=1,
                device_id={axis: here[axis] + step for axis, step in by.items()},
                device_id_type=pl.DeviceIdType.MESH,
            )

        partners = partners + valid.astype(jnp.int32)
    pl.when(first)(load_cache.start)
    load_weight.start()
    load_up.start()
    load_bias.start()
    load_up_bias.start()

    load_gain.wait()
    load_frames.wait()
    for f in range(count):
        for r in range(rows):
            x = fbuf[f, r].astype(F32)
            scale = lax.rsqrt(jnp.mean(x * x, axis=-1, keepdims=True) + EPS)
            v = x * scale * gain[...]
            ext[2 + f, 1 + r, 0:cols] = (v / (1.0 + jnp.exp(-v))).astype(BF16)

    @pl.when(ends["up"])
    def _():
        ext[:, 0, 0:cols] = jnp.zeros((2 + count, cols, channels), BF16)
        res[:, 0, 0:cols] = jnp.zeros((count, cols, channels), BF16)

    @pl.when(ends["down"])
    def _():
        ext[:, 1 + rows, 0:cols] = jnp.zeros((2 + count, cols, channels), BF16)
        res[:, 1 + rows, 0:cols] = jnp.zeros((count, cols, channels), BF16)

    index = 0

    def move(src, dst, by):
        nonlocal index
        made = Move(src, dst, sems, index, by)
        index += 1
        return made

    last = cols - EDGE

    def edges(buf, left, right, lo, hi):
        inside = slice(1, 1 + rows)
        near = slice(0, EDGE)
        far = slice(last, cols)
        across = [
            move(buf.at[lo:hi, 1, 0:cols], buf.at[lo:hi, 1 + rows, 0:cols], {"ha": -1}),
            move(buf.at[lo:hi, rows, 0:cols], buf.at[lo:hi, 0, 0:cols], {"ha": 1}),
        ]
        beside = [
            move(buf.at[lo:hi, 1, near], right.at[lo:hi, 1 + rows], {"ha": -1, "wa": -1}),
            move(buf.at[lo:hi, 1, far], left.at[lo:hi, 1 + rows], {"ha": -1, "wa": 1}),
            move(buf.at[lo:hi, rows, near], right.at[lo:hi, 0], {"ha": 1, "wa": -1}),
            move(buf.at[lo:hi, rows, far], left.at[lo:hi, 0], {"ha": 1, "wa": 1}),
            move(buf.at[lo:hi, inside, near], right.at[lo:hi, inside], {"wa": -1}),
            move(buf.at[lo:hi, inside, far], left.at[lo:hi, inside], {"wa": 1}),
        ]
        return across, beside

    def merge(buf, left, right, lo, hi):
        shape = (hi - lo, rows + 2, EDGE, channels)
        row = lax.broadcasted_iota(jnp.int32, shape, 1)
        at = lax.broadcasted_iota(jnp.int32, shape, 2)
        top = jnp.where(ends["up"], 1, 0)
        end = jnp.where(ends["down"], rows, rows + 1)
        held = jnp.logical_and(row >= top, row <= end)
        near = jnp.where(ends["right"], -1, 0)
        far = jnp.where(ends["left"], -1, EDGE - 1)
        tile = jnp.where(jnp.logical_and(held, at == far), left[lo:hi].astype(F32), 0.0)
        tile = jnp.where(jnp.logical_and(held, at == near), right[lo:hi].astype(F32), tile)
        buf[lo:hi, :, cols:wide] = tile.astype(BF16)

    def later(at, row, col):
        return move(ext.at[(at[0],) + (row, col)], ext.at[(at[1],) + (row, col)], {"ta": 1})

    both = (slice(2, 4), slice(0, 2))
    outer = [
        later(both, 1, slice(0, cols)),
        later(both, rows, slice(0, cols)),
        later(both, slice(2, rows), slice(0, EDGE)),
        later(both, slice(2, rows), slice(last, cols)),
    ]
    inner = {f: later((2 + f, f), slice(2, rows), slice(EDGE, last)) for f in (1, 0)}
    across_own, beside_own = edges(ext, lbuf, rbuf, 2, 4)
    across_old, beside_old = edges(ext, lbuf, rbuf, 0, 2)
    across_res, beside_res = {}, {}
    for o in (1, 0):
        across_res[o], beside_res[o] = edges(res, lbuf2, rbuf2, o, o + 1)

    def each(moves, name):
        for m in moves:
            getattr(m, name)()

    def window(buf, f, start, width):
        return buf[f, start : start + rows, 0:width].reshape(rows * width, channels)

    def center(terms):
        total = None
        for f, a in terms:
            for b in range(3):
                part = jnp.dot(
                    window(ext, f, b, cols), wbuf[9 * a + 3 * b + 1],
                    preferred_element_type=F32,
                )
                total = part if total is None else total + part
        return total

    def side(terms, c):
        total = None
        for f, a in terms:
            for b in range(3):
                part = jnp.dot(
                    window(ext, f, b, wide), wbuf[9 * a + 3 * b + c],
                    preferred_element_type=F32,
                )
                total = part if total is None else total + part
        return total

    own = {0: ((2, 2),), 1: ((2, 1), (3, 2))}

    pl.semaphore_wait(barrier, partners)
    each(outer, "start")
    each(across_own, "start")
    each(beside_own, "start")
    for f in (1, 0):
        inner[f].start()

    load_up.wait()
    load_bias.wait()
    load_up_bias.wait()
    u = {}
    for a in range(3):
        for b in range(3):
            u[a, b] = ubuf[3 * a + b].astype(F32)
    for p in range(2):
        for k in range(2):
            taps = PHASE_TAPS[p][k][1]
            by_col = [functools.reduce(jnp.add, [u[a, b] for a in taps]) for b in range(3)]
            folded[p, k, 0] = jnp.concatenate(
                [by_col[1] + by_col[2], by_col[0] + by_col[1]], axis=-1
            ).astype(BF16)
            folded[p, k, 1] = jnp.concatenate([by_col[0], by_col[2]], axis=-1).astype(BF16)

    pl.when(first)(load_cache.wait)
    for k in range(2):
        outer[k].recv()
        across_old[k].start()
    each(outer[2:], "recv")
    each(beside_old, "start")
    load_weight.wait()
    each(across_own, "recv")
    for o in (1, 0):
        mid[o] = center(own[o])
    each(beside_own, "recv")
    merge(ext, lbuf, rbuf, 2, 4)
    low[1] = side(own[1], 0)
    high[1] = side(own[1], 2)

    low[0] = side(own[0], 0)
    high[0] = side(own[0], 2)

    def finish(o, center_sum, low_sum, high_sum):
        for r in range(rows):
            span = slice(r * wide, (r + 1) * wide)
            total = center_sum[r * cols : (r + 1) * cols]
            total = total + pltpu.roll(low_sum[span], 1, 0)[0:cols]
            total = total + pltpu.roll(high_sum[span], wide - 1, 0)[0:cols]
            res[o, 1 + r, 0:cols] = (fbuf[o, r].astype(F32) + total + bias[...]).astype(BF16)

    inner[1].recv()
    each(across_old, "recv")
    mid[1] += center(((1, 0),))
    each(beside_old, "recv")
    merge(ext, lbuf, rbuf, 0, 2)
    low[1] += side(((1, 0),), 0)
    high[1] += side(((1, 0),), 2)
    finish(1, mid.at[1], low.at[1], high.at[1])
    each(across_res[1], "start")
    each(beside_res[1], "start")

    inner[0].recv()
    mid[0] += center(((1, 1), (0, 0)))
    low[0] += side(((1, 1), (0, 0)), 0)
    high[0] += side(((1, 1), (0, 0)), 2)
    finish(0, mid.at[0], low.at[0], high.at[0])
    each(across_res[0], "start")
    each(beside_res[0], "start")

    up = jnp.concatenate([up_bias[...], up_bias[...]], axis=-1)
    lane = lax.broadcasted_iota(jnp.int32, (wide, 2 * outputs), 1)

    def raised(o, p, kind, width):
        total = None
        for k in range(2):
            part = jnp.dot(
                window(res, o, PHASE_TAPS[p][k][0], width), folded[p, k, kind],
                preferred_element_type=F32,
            )
            total = part if total is None else total + part
        return total

    stores = {o: pltpu.make_async_copy(obuf.at[o], out.at[o], local_sems.at[7 + o]) for o in (1, 0)}
    for o in (1, 0):
        each(across_res[o], "recv")
        mid[o] = raised(o, 0, 0, cols)
        high[o, 0 : rows * cols] = raised(o, 1, 0, cols)
        each(beside_res[o], "recv")
        merge(res, lbuf2, rbuf2, o, o + 1)
        for p in range(2):
            total = raised(o, p, 1, wide)
            held = mid if p == 0 else high
            for r in range(rows):
                span = total[r * wide : (r + 1) * wide]
                turned = jnp.where(
                    lane < outputs, pltpu.roll(span, 1, 0), pltpu.roll(span, wide - 1, 0)
                )[0:cols]
                value = held[o, r * cols : (r + 1) * cols] + turned + up
                obuf[o, 2 * r + p] = value.astype(BF16)
        stores[o].start()

    each(outer, "sent")
    for f in (1, 0):
        inner[f].sent()
    for moves in (across_own, beside_own, across_old, beside_old):
        each(moves, "sent")
    for o in (1, 0):
        each(across_res[o], "sent")
        each(beside_res[o], "sent")
        stores[o].wait()


def on_device(frames, cache, norm_gain, conv_weight, conv_bias, up_weight, up_bias):
    count, rows, cols, channels = frames.shape
    outputs = up_weight.shape[-1]
    wide = cols + EDGE
    moves = 38
    hbm = pl.BlockSpec(memory_space=pltpu.HBM)
    return pl.pallas_call(
        kernel,
        out_shape=jax.ShapeDtypeStruct((count, 2 * rows, cols, 2 * outputs), BF16),
        in_specs=[hbm] * 7,
        out_specs=hbm,
        scratch_shapes=[
            pltpu.VMEM((count, rows, cols, channels), BF16),
            pltpu.VMEM((27, channels, channels), BF16),
            pltpu.VMEM((9, channels, outputs), BF16),
            pltpu.VMEM((1, channels), F32),
            pltpu.VMEM((1, channels), F32),
            pltpu.VMEM((1, outputs), F32),
            pltpu.VMEM((2, 2, 2, channels, 2 * outputs), BF16),
            pltpu.VMEM((2 + count, rows + 2, wide, channels), BF16),
            pltpu.VMEM((count, rows + 2, wide, channels), BF16),
            pltpu.VMEM((2 + count, rows + 2, EDGE, channels), BF16),
            pltpu.VMEM((2 + count, rows + 2, EDGE, channels), BF16),
            pltpu.VMEM((count, rows + 2, EDGE, channels), BF16),
            pltpu.VMEM((count, rows + 2, EDGE, channels), BF16),
            pltpu.VMEM((count, rows * cols, channels), F32),
            pltpu.VMEM((count, rows * wide, channels), F32),
            pltpu.VMEM((count, rows * wide, channels), F32),
            pltpu.VMEM((count, 2 * rows, cols, 2 * outputs), BF16),
            pltpu.SemaphoreType.DMA((9,)),
            pltpu.SemaphoreType.DMA((moves,)),
            pltpu.SemaphoreType.DMA((moves,)),
        ],
        compiler_params=pltpu.CompilerParams(
            collective_id=0, has_side_effects=True, vmem_limit_bytes=65_000_000
        ),
        name="level",
    )(
        frames,
        cache,
        norm_gain.reshape(1, channels),
        conv_weight.reshape(27, channels, channels),
        conv_bias.reshape(1, channels),
        up_weight.reshape(9, channels, outputs),
        up_bias.reshape(1, outputs),
    )


def solution(mesh):
    return jax.shard_map(
        on_device,
        mesh=mesh,
        in_specs=(
            P(("clips", "ta"), "ha", "wa", None),
            P("clips", "ha", "wa", None),
            P(),
            P(),
            P(),
            P(),
            P(),
        ),
        out_specs=P(("clips", "ta"), "ha", "wa", None),
        check_vma=False,
    )
```

```python
import functools

import jax
import jax.numpy as jnp
from jax import lax
from jax.experimental import pallas as pl
from jax.experimental.pallas import tpu as pltpu
from jax.sharding import PartitionSpec as P

EPS = 1e-06
EDGE = 16
PHASE_TAPS = (((0, (0,)), (1, (1, 2))), ((1, (0, 1)), (2, (2,))))
NEIGHBOURS = (
    {"ta": 1}, {"ta": -1}, {"ha": 1}, {"ha": -1}, {"wa": 1}, {"wa": -1},
    {"ha": 1, "wa": 1}, {"ha": 1, "wa": -1}, {"ha": -1, "wa": 1}, {"ha": -1, "wa": -1},
)
F32 = jnp.float32
BF16 = jnp.bfloat16


def reachable(by, sign):
    found = None
    for axis, step in by.items():
        there = lax.axis_index(axis) + sign * step
        inside = jnp.logical_and(there >= 0, there < lax.axis_size(axis))
        found = inside if found is None else jnp.logical_and(found, inside)
    return found


class Move:
    def __init__(self, src, dst, sems, index, by):
        self.can_send = reachable(by, 1)
        self.can_recv = reachable(by, -1)
        self.copy = lambda: pltpu.make_async_remote_copy(
            src_ref=src,
            dst_ref=dst,
            send_sem=sems[0].at[index],
            recv_sem=sems[1].at[index],
            device_id={axis: lax.axis_index(axis) + step for axis, step in by.items()},
            device_id_type=pl.DeviceIdType.MESH,
        )

    def start(self):
        pl.when(self.can_send)(lambda: self.copy().start())

    def recv(self):
        pl.when(self.can_recv)(lambda: self.copy().wait_recv())

    def sent(self):
        pl.when(self.can_send)(lambda: self.copy().wait_send())


def kernel(
    frames, cache, gain_in, weight, bias_in, up_weight, up_bias_in, out,
    fbuf, wbuf, ubuf, gain, bias, up_bias, folded, ext, res, lbuf, rbuf, lbuf2, rbuf2, mid, low, high, obuf,
    local_sems, send_sems, recv_sems,
):
    count, rows, cols, channels = fbuf.shape
    wide = cols + EDGE
    outputs = ubuf.shape[-1]
    sems = (send_sems, recv_sems)
    here = {axis: lax.axis_index(axis) for axis in ("ta", "ha", "wa")}
    first = here["ta"] == 0
    ends = {
        "up": here["ha"] == 0,
        "down": here["ha"] == lax.axis_size("ha") - 1,
        "left": here["wa"] == 0,
        "right": here["wa"] == lax.axis_size("wa") - 1,
    }

    load_frames = pltpu.make_async_copy(frames, fbuf, local_sems.at[0])
    load_weight = pltpu.make_async_copy(weight, wbuf, local_sems.at[1])
    load_up = pltpu.make_async_copy(up_weight, ubuf, local_sems.at[2])
    load_cache = pltpu.make_async_copy(
        cache, ext.at[0:2, 1 : 1 + rows, 0:cols], local_sems.at[3]
    )
    load_gain = pltpu.make_async_copy(gain_in, gain, local_sems.at[4])
    load_bias = pltpu.make_async_copy(bias_in, bias, local_sems.at[5])
    load_up_bias = pltpu.make_async_copy(up_bias_in, up_bias, local_sems.at[6])
    load_frames.start()
    load_gain.start()
    barrier = pltpu.get_barrier_semaphore()
    partners = jnp.int32(0)
    for by in NEIGHBOURS:
        valid = reachable(by, 1)

        @pl.when(valid)
        def _():
            pl.semaphore_signal(
                barrier, inc=1,
                device_id={axis: here[axis] + step for axis, step in by.items()},
                device_id_type=pl.DeviceIdType.MESH,
            )

        partners = partners + valid.astype(jnp.int32)
    pl.when(first)(load_cache.start)
    load_weight.start()
    load_up.start()
    load_bias.start()
    load_up_bias.start()

    load_gain.wait()
    load_frames.wait()
    def activate(f, r):
        x = fbuf[f, r].astype(F32)
        scale = lax.rsqrt(jnp.mean(x * x, axis=-1, keepdims=True) + EPS)
        v = x * scale * gain[...]
        ext[2 + f, 1 + r, 0:cols] = (v / (1.0 + jnp.exp(-v))).astype(BF16)

    for f in range(count):
        for r in (0, rows - 1):
            activate(f, r)

    @pl.when(ends["up"])
    def _():
        ext[:, 0, 0:cols] = jnp.zeros((2 + count, cols, channels), BF16)
        res[:, 0, 0:cols] = jnp.zeros((count, cols, channels), BF16)

    @pl.when(ends["down"])
    def _():
        ext[:, 1 + rows, 0:cols] = jnp.zeros((2 + count, cols, channels), BF16)
        res[:, 1 + rows, 0:cols] = jnp.zeros((count, cols, channels), BF16)

    index = 0

    def move(src, dst, by):
        nonlocal index
        made = Move(src, dst, sems, index, by)
        index += 1
        return made

    last = cols - EDGE

    def edges(buf, left, right, lo, hi):
        inside = slice(1, 1 + rows)
        near = slice(0, EDGE)
        far = slice(last, cols)
        across = [
            move(buf.at[lo:hi, 1, 0:cols], buf.at[lo:hi, 1 + rows, 0:cols], {"ha": -1}),
            move(buf.at[lo:hi, rows, 0:cols], buf.at[lo:hi, 0, 0:cols], {"ha": 1}),
        ]
        beside = [
            move(buf.at[lo:hi, 1, near], right.at[lo:hi, 1 + rows], {"ha": -1, "wa": -1}),
            move(buf.at[lo:hi, 1, far], left.at[lo:hi, 1 + rows], {"ha": -1, "wa": 1}),
            move(buf.at[lo:hi, rows, near], right.at[lo:hi, 0], {"ha": 1, "wa": -1}),
            move(buf.at[lo:hi, rows, far], left.at[lo:hi, 0], {"ha": 1, "wa": 1}),
            move(buf.at[lo:hi, inside, near], right.at[lo:hi, inside], {"wa": -1}),
            move(buf.at[lo:hi, inside, far], left.at[lo:hi, inside], {"wa": 1}),
        ]
        return across, beside

    def merge(buf, left, right, lo, hi):
        shape = (hi - lo, rows + 2, EDGE, channels)
        row = lax.broadcasted_iota(jnp.int32, shape, 1)
        at = lax.broadcasted_iota(jnp.int32, shape, 2)
        top = jnp.where(ends["up"], 1, 0)
        end = jnp.where(ends["down"], rows, rows + 1)
        held = jnp.logical_and(row >= top, row <= end)
        near = jnp.where(ends["right"], -1, 0)
        far = jnp.where(ends["left"], -1, EDGE - 1)
        tile = jnp.where(jnp.logical_and(held, at == far), left[lo:hi].astype(F32), 0.0)
        tile = jnp.where(jnp.logical_and(held, at == near), right[lo:hi].astype(F32), tile)
        buf[lo:hi, :, cols:wide] = tile.astype(BF16)

    def later(at, row, col):
        return move(ext.at[(at[0],) + (row, col)], ext.at[(at[1],) + (row, col)], {"ta": 1})

    both = (slice(2, 4), slice(0, 2))
    outer = [
        later(both, 1, slice(0, cols)),
        later(both, rows, slice(0, cols)),
        later(both, slice(2, rows), slice(0, EDGE)),
        later(both, slice(2, rows), slice(last, cols)),
    ]
    inner = {f: later((2 + f, f), slice(2, rows), slice(EDGE, last)) for f in (1, 0)}
    across_own, beside_own = edges(ext, lbuf, rbuf, 2, 4)
    across_old, beside_old = edges(ext, lbuf, rbuf, 0, 2)
    across_res, beside_res = {}, {}
    for o in (1, 0):
        across_res[o], beside_res[o] = edges(res, lbuf2, rbuf2, o, o + 1)

    def each(moves, name):
        for m in moves:
            getattr(m, name)()

    def window(buf, f, start, width):
        return buf[f, start : start + rows, 0:width].reshape(rows * width, channels)

    def center(terms):
        total = None
        for f, a in terms:
            for b in range(3):
                part = jnp.dot(
                    window(ext, f, b, cols), wbuf[9 * a + 3 * b + 1],
                    preferred_element_type=F32,
                )
                total = part if total is None else total + part
        return total

    def side(terms, c):
        total = None
        for f, a in terms:
            for b in range(3):
                part = jnp.dot(
                    window(ext, f, b, wide), wbuf[9 * a + 3 * b + c],
                    preferred_element_type=F32,
                )
                total = part if total is None else total + part
        return total

    own = {0: ((2, 2),), 1: ((2, 1), (3, 2))}

    pl.semaphore_wait(barrier, partners)
    each(outer[:2], "start")
    each(across_own, "start")
    each(beside_own[:4], "start")
    for f in range(count):
        for r in range(1, rows - 1):
            activate(f, r)
    each(outer[2:], "start")
    each(beside_own[4:], "start")
    for f in (1, 0):
        inner[f].start()

    load_up.wait()
    load_bias.wait()
    load_up_bias.wait()
    u = {}
    for a in range(3):
        for b in range(3):
            u[a, b] = ubuf[3 * a + b].astype(F32)
    for p in range(2):
        for k in range(2):
            taps = PHASE_TAPS[p][k][1]
            by_col = [functools.reduce(jnp.add, [u[a, b] for a in taps]) for b in range(3)]
            folded[p, k, 0] = jnp.concatenate(
                [by_col[1] + by_col[2], by_col[0] + by_col[1]], axis=-1
            ).astype(BF16)
            folded[p, k, 1] = jnp.concatenate([by_col[0], by_col[2]], axis=-1).astype(BF16)

    pl.when(first)(load_cache.wait)
    for k in range(2):
        outer[k].recv()
        across_old[k].start()
    each(outer[2:], "recv")
    each(beside_old, "start")
    load_weight.wait()
    each(across_own, "recv")
    for o in (1, 0):
        mid[o] = center(own[o])
    each(beside_own, "recv")
    merge(ext, lbuf, rbuf, 2, 4)
    low[1] = side(own[1], 0)
    high[1] = side(own[1], 2)

    low[0] = side(own[0], 0)
    high[0] = side(own[0], 2)

    def finish(o, center_sum, low_sum, high_sum):
        for r in range(rows):
            span = slice(r * wide, (r + 1) * wide)
            total = center_sum[r * cols : (r + 1) * cols]
            total = total + pltpu.roll(low_sum[span], 1, 0)[0:cols]
            total = total + pltpu.roll(high_sum[span], wide - 1, 0)[0:cols]
            res[o, 1 + r, 0:cols] = (fbuf[o, r].astype(F32) + total + bias[...]).astype(BF16)

    inner[1].recv()
    each(across_old, "recv")
    mid[1] += center(((1, 0),))
    each(beside_old, "recv")
    merge(ext, lbuf, rbuf, 0, 2)
    low[1] += side(((1, 0),), 0)
    high[1] += side(((1, 0),), 2)
    finish(1, mid.at[1], low.at[1], high.at[1])
    each(across_res[1], "start")
    each(beside_res[1], "start")

    inner[0].recv()
    mid[0] += center(((1, 1), (0, 0)))
    low[0] += side(((1, 1), (0, 0)), 0)
    high[0] += side(((1, 1), (0, 0)), 2)
    finish(0, mid.at[0], low.at[0], high.at[0])
    each(across_res[0], "start")
    each(beside_res[0], "start")

    up = jnp.concatenate([up_bias[...], up_bias[...]], axis=-1)
    lane = lax.broadcasted_iota(jnp.int32, (wide, 2 * outputs), 1)

    def raised(o, p, kind, width):
        total = None
        for k in range(2):
            part = jnp.dot(
                window(res, o, PHASE_TAPS[p][k][0], width), folded[p, k, kind],
                preferred_element_type=F32,
            )
            total = part if total is None else total + part
        return total

    stores = {o: pltpu.make_async_copy(obuf.at[o], out.at[o], local_sems.at[7 + o]) for o in (1, 0)}
    for o in (1, 0):
        each(across_res[o], "recv")
        mid[o] = raised(o, 0, 0, cols)
        high[o, 0 : rows * cols] = raised(o, 1, 0, cols)
        each(beside_res[o], "recv")
        merge(res, lbuf2, rbuf2, o, o + 1)
        for p in range(2):
            total = raised(o, p, 1, wide)
            held = mid if p == 0 else high
            for r in range(rows):
                span = total[r * wide : (r + 1) * wide]
                turned = jnp.where(
                    lane < outputs, pltpu.roll(span, 1, 0), pltpu.roll(span, wide - 1, 0)
                )[0:cols]
                value = held[o, r * cols : (r + 1) * cols] + turned + up
                obuf[o, 2 * r + p] = value.astype(BF16)
        stores[o].start()

    each(outer, "sent")
    for f in (1, 0):
        inner[f].sent()
    for moves in (across_own, beside_own, across_old, beside_old):
        each(moves, "sent")
    for o in (1, 0):
        each(across_res[o], "sent")
        each(beside_res[o], "sent")
        stores[o].wait()


def on_device(frames, cache, norm_gain, conv_weight, conv_bias, up_weight, up_bias):
    count, rows, cols, channels = frames.shape
    outputs = up_weight.shape[-1]
    wide = cols + EDGE
    moves = 38
    hbm = pl.BlockSpec(memory_space=pltpu.HBM)
    return pl.pallas_call(
        kernel,
        out_shape=jax.ShapeDtypeStruct((count, 2 * rows, cols, 2 * outputs), BF16),
        in_specs=[hbm] * 7,
        out_specs=hbm,
        scratch_shapes=[
            pltpu.VMEM((count, rows, cols, channels), BF16),
            pltpu.VMEM((27, channels, channels), BF16),
            pltpu.VMEM((9, channels, outputs), BF16),
            pltpu.VMEM((1, channels), F32),
            pltpu.VMEM((1, channels), F32),
            pltpu.VMEM((1, outputs), F32),
            pltpu.VMEM((2, 2, 2, channels, 2 * outputs), BF16),
            pltpu.VMEM((2 + count, rows + 2, wide, channels), BF16),
            pltpu.VMEM((count, rows + 2, wide, channels), BF16),
            pltpu.VMEM((2 + count, rows + 2, EDGE, channels), BF16),
            pltpu.VMEM((2 + count, rows + 2, EDGE, channels), BF16),
            pltpu.VMEM((count, rows + 2, EDGE, channels), BF16),
            pltpu.VMEM((count, rows + 2, EDGE, channels), BF16),
            pltpu.VMEM((count, rows * cols, channels), F32),
            pltpu.VMEM((count, rows * wide, channels), F32),
            pltpu.VMEM((count, rows * wide, channels), F32),
            pltpu.VMEM((count, 2 * rows, cols, 2 * outputs), BF16),
            pltpu.SemaphoreType.DMA((9,)),
            pltpu.SemaphoreType.DMA((moves,)),
            pltpu.SemaphoreType.DMA((moves,)),
        ],
        compiler_params=pltpu.CompilerParams(
            collective_id=0, has_side_effects=True, vmem_limit_bytes=65_000_000
        ),
        name="level",
    )(
        frames,
        cache,
        norm_gain.reshape(1, channels),
        conv_weight.reshape(27, channels, channels),
        conv_bias.reshape(1, channels),
        up_weight.reshape(9, channels, outputs),
        up_bias.reshape(1, outputs),
    )


def solution(mesh):
    return jax.shard_map(
        on_device,
        mesh=mesh,
        in_specs=(
            P(("clips", "ta"), "ha", "wa", None),
            P("clips", "ha", "wa", None),
            P(),
            P(),
            P(),
            P(),
            P(),
        ),
        out_specs=P(("clips", "ta"), "ha", "wa", None),
        check_vma=False,
    )
```
